32 devices in a mesh: groups: 2 (over x), rows: 16 (over z, y, core).
Axes of the slice: x: 2, y: 2, z: 4, core: 2. Of those that a mesh axis runs over, the one named last changes fastest.
Arguments:
- in_acts: bfloat16 [512, 14336], P(('groups', 'rows')), parts along dimension 0, may hold values from -6 to 6
- out_grads: bfloat16 [512, 4096], P(('groups', 'rows')), parts along dimension 0, may hold values from -6 to 6
- in_projection: bfloat16 [128, 14336], replicated, may hold values from -0.046875 to 0.046875
- out_projection: bfloat16 [128, 4096], replicated, may hold values from -0.09375 to 0.09375
- inverse: bfloat16 [16384, 16384], P('rows'), as said below
- stored_rows: bfloat16 [1536, 16384], P(('groups', 'rows')), parts along dimension 0, may hold values from -0.0078125 to 0.0078125
- query_ids: int32 [512], P(('groups', 'rows')), parts along dimension 0, may hold values from 0 to 15, never falling along the last dimension, each value on 1 to 32 neighbouring positions
- example_ids: int32 [32, 48], P(('groups', 'rows')), parts along dimension 0, may hold values from 0 to 15, never falling along the last dimension, each value on 1 to 8 neighbouring positions
Outputs:
- example_scores: float32 [512, 16], P(('groups', 'rows')), parts along dimension 0
The draws below stay inside these ranges and needn't reach their ends.
There are 2 independent parts, one for each index of `groups`. The reference program is written for one: setup_inputs(seed, part) draws one part's arguments, and reference() takes and returns one part's arrays. A program takes and returns all parts, laid end to end along the dimension named above; an argument that names none is the same for every part. Nothing has to cross between parts.
Inputs may be any that keep to these rules, and one draw needn't show every extreme that they name: `query_ids`: tokens of one query stand together, queries in increasing order; a query may span several devices. `example_ids`: within each block, rows of one example stand together in increasing order, each example with at least one row. `inverse`: the matrix is exactly symmetric.
All inputs are finite; a program needn't handle non-finite values.
Results may differ from the reference program's by a relative error of at most 0.0057.
Values may be sent and summed in bfloat16 or wider, within the bound.
No kernel may reach another device: no remote copies, remote signals or barrier semaphores. Data moves between devices by JAX's collectives and lax.ppermute only.
A program may use at most 128 MiB of HBM per device.

```python
import math
import jax
import jax.numpy as jnp
import numpy as np
from jax import lax

D = 4096
FF = 14336
KIN = 128
KOUT = 128
QRY_DEV = 1
TOK_DEV = 16
STORE_DEV = 48
EX_DEV = 16
COORDS = 16384
QUERIES = 16
TOKENS = 256
SHARDS = 16
STORE = 768


def draw_inverse(key, part):
    first_key, second_key = jax.random.split(jax.random.fold_in(key, 7))
    noise = jax.random.normal(first_key, (COORDS, COORDS), jnp.float32)
    symmetric = (noise + noise.T) * (0.35 / math.sqrt(2.0 * COORDS))
    diagonal = jnp.exp(jax.random.uniform(second_key, (COORDS,), jnp.float32, 0.0, math.log(2.0)))
    return (symmetric + jnp.diag(diagonal)).astype(jnp.bfloat16)


def levels(own_key, extent, cuts, smallest, high):
    def one(dim, parts):
        steps = jax.random.uniform(jax.random.fold_in(jax.random.fold_in(own_key, 6), dim), (parts,), jnp.float32, smallest / len(cuts), high / len(cuts))
        return jnp.repeat(jnp.exp(steps), extent[dim] // parts).reshape((-1,) + (1,) * (len(extent) - dim - 1))

    level = one(*cuts[0])
    for cut in cuts[1:]:
        level = level * one(*cut)
    return level


def split_up(number_of, total, bound, skew):
    portions = [(1 << 20) // math.isqrt(grade ** skew) + 1 for grade in range(2, number_of + 1)]
    surplus, holding = total - bound - (number_of - 1), [1] * (number_of - 1)
    while surplus > 0:
        movable = [i for i in range(number_of - 1) if holding[i] < bound]
        pool, left = sum([portions[i] for i in movable]), surplus
        for i in movable:
            more = min(bound - holding[i], max(1, left * portions[i] // pool), surplus)
            holding[i] = holding[i] + more
            surplus = surplus - more
    return np.array([bound] + holding)


def uneven(stream_key, amount, total, bound, lean):
    if amount == 2:
        one = jax.random.randint(stream_key, (), max(1, total - bound), min(bound, total - 1) + 1)
        return jnp.stack([one, total - one])
    lengths = jnp.asarray(split_up(amount, total, bound, lean), jnp.int32)
    couples = (amount - 1) // 2
    giver, taker = lengths[1:1 + 2 * couples:2], lengths[2:2 + 2 * couples:2]
    margin = jnp.minimum(giver - 1, bound - taker)
    shifted = jax.random.randint(jax.random.fold_in(stream_key, 1), (couples,), 0, 1 << 20) % (margin + 1)
    lengths = lengths.at[1:1 + 2 * couples:2].set(giver - shifted).at[2:2 + 2 * couples:2].set(taker + shifted)
    return lengths[jax.random.permutation(jax.random.fold_in(stream_key, 2), amount)]


def scatter_about(stream_key, extent, width, most, cuts=(), kind=jnp.bfloat16):
    level = levels(stream_key, extent, cuts, -0.22, 0.18) if cuts else 1.0
    values = jax.random.normal(stream_key, extent, jnp.float32) * width * level
    return jnp.minimum(jnp.maximum(values, -most), most).astype(kind)


def setup_inputs(seed: int = 0, part: int = 0) -> dict:
    key_list = jax.random.split(jax.random.key(seed), 9)
    own_keys = jax.random.split(jax.random.fold_in(key_list[8], part), 9)
    in_acts = scatter_about(own_keys[0], (TOKENS, FF), 1.0, 6.0, ((0, 16),))
    out_grads = scatter_about(own_keys[1], (TOKENS, D), 1.0, 6.0, ((0, 16),))
    in_projection = scatter_about(key_list[2], (KIN, FF), FF ** -0.5, 0.046875)
    out_projection = scatter_about(key_list[3], (KOUT, D), D ** -0.5, 0.09375)
    inverse = draw_inverse(jax.random.fold_in(key_list[8], 71), part)
    stored_rows = scatter_about(own_keys[5], (STORE, COORDS), (32 * COORDS) ** -0.5, 0.0078125, ((0, 16),))
    query_ids = jnp.searchsorted(jnp.cumsum(uneven(own_keys[6], QUERIES, TOKENS, 2 * TOK_DEV // QRY_DEV, 1)), jnp.arange(TOKENS), side="right").astype(jnp.int32)
    example_ids = jax.vmap(lambda own: jnp.searchsorted(jnp.cumsum(uneven(own, EX_DEV, STORE_DEV, min(8, STORE_DEV - EX_DEV + 1), 1)), jnp.arange(STORE_DEV), side="right"))(jax.random.split(own_keys[7], SHARDS)).reshape((SHARDS, STORE_DEV)).astype(jnp.int32)
    return dict(in_acts=in_acts, out_grads=out_grads, in_projection=in_projection, out_projection=out_projection, inverse=inverse, stored_rows=stored_rows, query_ids=query_ids, example_ids=example_ids)


def reference(in_acts, out_grads, in_projection, out_projection, inverse, stored_rows, query_ids, example_ids):
    in_proj = lax.dot_general(in_acts, in_projection, (((1,), (1,)), ((), ())), preferred_element_type=jnp.float32).astype(jnp.bfloat16)
    out_proj = lax.dot_general(out_grads, out_projection, (((1,), (1,)), ((), ())), preferred_element_type=jnp.float32).astype(jnp.bfloat16)
    member = (query_ids[:, None] == jnp.arange(QUERIES, dtype=jnp.int32)[None, :]).astype(jnp.float32)
    weighted = (member[:, :, None] * out_proj.astype(jnp.float32)[:, None, :]).reshape(TOKENS, QUERIES * KOUT)
    grads_full = jnp.dot(weighted.T, in_proj.astype(jnp.float32), precision=lax.Precision.HIGHEST)
    query_grads = grads_full.reshape(QUERIES, KOUT * KIN).astype(jnp.bfloat16)
    precond = jnp.dot(query_grads, inverse, preferred_element_type=jnp.float32).astype(jnp.bfloat16)
    row_scores = lax.dot_general(stored_rows, precond, (((1,), (1,)), ((), ())), preferred_element_type=jnp.float32)
    blocked = row_scores.reshape(SHARDS, STORE_DEV, QUERIES)
    example_member = (example_ids[:, :, None] == jnp.arange(EX_DEV, dtype=jnp.int32)[None, None, :]).astype(jnp.float32)
    summed = jnp.einsum("bse,bsq->beq", example_member, blocked, precision=lax.Precision.HIGHEST)
    return summed.reshape(SHARDS * EX_DEV, QUERIES)
```

```python
import functools

import jax
import jax.numpy as jnp
from jax import lax
from jax.experimental import pallas as pl
from jax.experimental.pallas import tpu as pltpu
from jax.sharding import PartitionSpec as P

LANES = 128
QRY_DEV = 1
EX_DEV = 16
NT = (((1,), (1,)), ((), ()))
VMEM = pl.BlockSpec(memory_space=pltpu.VMEM)
ANY = pl.BlockSpec(memory_space=pl.ANY)


def chunk_of(total, most):
    size = most
    while total % size:
        size //= 2
    return size


def round_up(n, m):
    return -(-n // m) * m


def project_kernel(acts, grads, in_w, out_w, ids, tok, acts_v, grads_v, in_v, out_v, sem, *, step):
    pieces = [(grads, grads_v, out_w, out_v, 0, grads.shape[1])]
    pieces += [(acts, acts_v, in_w, in_v, k, step) for k in range(0, acts.shape[1], step)]
    copies = []
    for n, (x, x_v, w, w_v, k, size) in enumerate(pieces):
        cols = pl.ds(k, size)
        copies.append(
            (
                pltpu.make_async_copy(x.at[:, cols], x_v.at[:, cols], sem.at[n, 0]),
                pltpu.make_async_copy(w.at[:, cols], w_v.at[:, cols], sem.at[n, 1]),
            )
        )
    for pair in copies:
        for copy in pair:
            copy.start()
    tokens, kin = acts.shape[0], in_w.shape[0]
    kout, width = out_w.shape[0], tok.shape[1] - in_w.shape[0] - out_w.shape[0]
    row = lax.broadcasted_iota(jnp.int32, (tokens, tokens), 0)
    col = lax.broadcasted_iota(jnp.int32, (tokens, tokens), 1)
    mine = jnp.sum(jnp.where(row == col, ids[...], 0), axis=1, keepdims=True)
    query = lax.broadcasted_iota(jnp.int32, (tokens, width), 1)
    tok[:, kin + kout :] = jnp.where(query == mine, 1.0, 0.0).astype(jnp.bfloat16)
    total = jnp.zeros((tokens, kin), jnp.float32)
    for n, (x, x_v, w, w_v, k, size) in enumerate(pieces):
        for copy in copies[n]:
            copy.wait()
        part = lax.dot_general(
            x_v[:, k : k + size], w_v[:, k : k + size], NT, preferred_element_type=jnp.float32
        )
        if n == 0:
            tok[:, kin : kin + kout] = part.astype(jnp.bfloat16)
        else:
            total += part
    tok[:, :kin] = total.astype(jnp.bfloat16)


def project(acts, grads, in_w, out_w, ids, queries):
    tokens, ff = acts.shape
    step = chunk_of(ff, 2048)
    width = in_w.shape[0] + out_w.shape[0] + round_up(queries, LANES)
    return pl.pallas_call(
        functools.partial(project_kernel, step=step),
        in_specs=[ANY] * 4 + [VMEM],
        out_specs=VMEM,
        out_shape=jax.ShapeDtypeStruct((tokens, width), jnp.bfloat16),
        scratch_shapes=[
            pltpu.VMEM(acts.shape, acts.dtype),
            pltpu.VMEM(grads.shape, grads.dtype),
            pltpu.VMEM(in_w.shape, in_w.dtype),
            pltpu.VMEM(out_w.shape, out_w.dtype),
            pltpu.SemaphoreType.DMA((ff // step + 1, 2)),
        ],
        compiler_params=pltpu.CompilerParams(vmem_limit_bytes=8 << 20),
        name="project",
    )(acts, grads, in_w, out_w, ids)


def precond_kernel(tok, inverse, out, out_t, member_t, acc, *, kin, kout, per, queries):
    out_t[...] = tok[:, kin : kin + kout].astype(jnp.float32).T.astype(jnp.bfloat16)
    member_t[...] = (
        tok[:, kin + kout :].astype(jnp.float32).T[:queries].astype(jnp.bfloat16)
    )
    acc[...] = jnp.zeros_like(acc)

    def step(s):
        o = out_t[pl.ds(pl.multiple_of(s * per, per), per), :]
        weighted = (o[:, None, :] * member_t[...][None, :, :]).reshape(per * queries, o.shape[1])
        g = jnp.dot(weighted, tok[:, :kin], preferred_element_type=jnp.float32)
        g = g.astype(jnp.bfloat16)
        g = jnp.concatenate([g[k * queries : (k + 1) * queries] for k in range(per)], axis=1)
        block = inverse[:, pl.ds(pl.multiple_of(s * per * kin, per * kin), per * kin)]
        acc[...] += lax.dot_general(g, block, NT, preferred_element_type=jnp.float32)

    pl.loop(0, kout // per)(step)
    out[...] = acc[...].astype(jnp.bfloat16)


def precondition(tok, inverse, kin, kout, queries):
    rows, coords = inverse.shape
    tokens = tok.shape[0]
    per = chunk_of(kout, 16)
    return pl.pallas_call(
        functools.partial(precond_kernel, kin=kin, kout=kout, per=per, queries=queries),
        in_specs=[VMEM, VMEM],
        out_specs=VMEM,
        out_shape=jax.ShapeDtypeStruct((queries, rows), jnp.bfloat16),
        scratch_shapes=[
            pltpu.VMEM((kout, tokens), jnp.bfloat16),
            pltpu.VMEM((queries, tokens), jnp.bfloat16),
            pltpu.VMEM((queries, rows), jnp.float32),
        ],
        compiler_params=pltpu.CompilerParams(vmem_limit_bytes=16 << 20),
        cost_estimate=pl.CostEstimate(
            flops=2 * queries * rows * coords,
            bytes_accessed=2 * rows * coords,
            transcendentals=0,
        ),
        name="precondition",
    )(tok, inverse)


def score_kernel(near, far, stored, ids, out, *, masks, axis):
    me = lax.axis_index(axis)
    rows = near.shape[2]
    scores = jnp.zeros((stored.shape[0], near.shape[1]), jnp.float32)
    half = len(masks) // 2
    for n, mask in enumerate(masks):
        block = near[n] if n < half else far[n - half]
        start = pl.multiple_of((me ^ mask) * rows, rows)
        scores += lax.dot_general(
            stored[:, pl.ds(start, rows)], block, NT, preferred_element_type=jnp.float32
        )
    example = lax.broadcasted_iota(jnp.int32, (out.shape[0], ids.shape[1]), 0)
    member = jnp.where(example == ids[...], 1.0, 0.0)
    out[...] = jnp.dot(
        member, scores, precision=lax.Precision.HIGHEST, preferred_element_type=jnp.float32
    )


def score(near, far, stored, ids, masks, queries):
    return pl.pallas_call(
        functools.partial(score_kernel, masks=masks, axis="rows"),
        in_specs=[VMEM] * 4,
        out_specs=VMEM,
        out_shape=jax.ShapeDtypeStruct((EX_DEV, queries), jnp.float32),
        compiler_params=pltpu.CompilerParams(vmem_limit_bytes=8 << 20),
        name="score",
    )(near, far, stored, ids)


def stages_of(n):
    bits = []
    bit = n // 2
    while bit:
        bits.append(bit)
        bit //= 2
    return bits


def swap(x, bit, n):
    return lax.ppermute(x, "rows", [(i, i ^ bit) for i in range(n)])


def on_device(
    in_acts, out_grads, in_projection, out_projection, inverse, stored_rows, query_ids, example_ids
):
    n = lax.axis_size("rows")
    bits = stages_of(n)
    queries = QRY_DEV * n
    kin, kout = in_projection.shape[0], out_projection.shape[0]
    tok = project(
        in_acts, out_grads, in_projection, out_projection, query_ids[None, :], queries
    )
    inverse, tok = lax.optimization_barrier((inverse, tok))
    for bit in bits:
        tok = jnp.concatenate([tok, swap(tok, bit, n)], axis=0)
    near = precondition(tok, inverse, kin, kout, queries)[None]
    masks = [0]
    for bit in bits:
        masks += [m ^ bit for m in masks]
        far = swap(near, bit, n)
        if bit != bits[-1]:
            near = jnp.concatenate([near, far], axis=0)
    return score(near, far, stored_rows, example_ids, masks, queries)


def solution(mesh):
    placed = (
        P(("groups", "rows"), None),
        P(("groups", "rows"), None),
        P(),
        P(),
        P("rows", None),
        P(("groups", "rows"), None),
        P(("groups", "rows")),
        P(("groups", "rows"), None),
    )
    return jax.shard_map(
        on_device,
        mesh=mesh,
        in_specs=placed,
        out_specs=P(("groups", "rows"), None),
        check_vma=False,
    )
```

```python
import functools

import jax
import jax.numpy as jnp
from jax import lax
from jax.experimental import pallas as pl
from jax.experimental.pallas import tpu as pltpu
from jax.sharding import PartitionSpec as P

LANES = 128
QRY_DEV = 1
EX_DEV = 16
NT = (((1,), (1,)), ((), ()))
VMEM = pl.BlockSpec(memory_space=pltpu.VMEM)
ANY = pl.BlockSpec(memory_space=pl.ANY)
VMEM_BYTES = 67_043_328 - (1 << 16)


def chunk_of(total, most):
    size = most
    while total % size:
        size //= 2
    return size


def round_up(n, m):
    return -(-n // m) * m


def project_kernel(acts, grads, in_w, out_w, raw, acts_v, grads_v, in_v, out_v, sem, *, step):
    pieces = [(grads, grads_v, out_w, out_v, 0, grads.shape[1])]
    pieces += [(acts, acts_v, in_w, in_v, k, step) for k in range(0, acts.shape[1], step)]
    copies = []
    for n, (x, x_v, w, w_v, k, size) in enumerate(pieces):
        cols = pl.ds(k, size)
        copies.append(
            (
                pltpu.make_async_copy(x.at[:, cols], x_v.at[:, cols], sem.at[n, 0]),
                pltpu.make_async_copy(w.at[:, cols], w_v.at[:, cols], sem.at[n, 1]),
            )
        )
    for pair in copies:
        for copy in pair:
            copy.start()
    kin = in_w.shape[0]
    total = None
    for n, (x, x_v, w, w_v, k, size) in enumerate(pieces):
        for copy in copies[n]:
            copy.wait()
        part = lax.dot_general(
            x_v[:, k : k + size], w_v[:, k : k + size], NT, preferred_element_type=jnp.float32
        )
        if n == 0:
            raw[:, kin:] = part.astype(jnp.bfloat16)
        else:
            total = part if total is None else total + part
    raw[:, :kin] = total.astype(jnp.bfloat16)


def mark_kernel(raw, ids, tok):
    tokens, done = raw.shape
    row = lax.broadcasted_iota(jnp.int32, (tokens, tokens), 0)
    col = lax.broadcasted_iota(jnp.int32, (tokens, tokens), 1)
    mine = jnp.sum(jnp.where(row == col, ids[...], 0), axis=1, keepdims=True)
    query = lax.broadcasted_iota(jnp.int32, (tokens, tok.shape[1] - done), 1)
    tok[:, :done] = raw[...]
    tok[:, done:] = jnp.where(query == mine, 1.0, 0.0).astype(jnp.bfloat16)


def project(acts, grads, in_w, out_w, ids, queries):
    tokens, ff = acts.shape
    step = chunk_of(ff, 2048)
    width = in_w.shape[0] + out_w.shape[0]
    raw = pl.pallas_call(
        functools.partial(project_kernel, step=step),
        in_specs=[ANY] * 4,
        out_specs=VMEM,
        out_shape=jax.ShapeDtypeStruct((tokens, width), jnp.bfloat16),
        scratch_shapes=[
            pltpu.VMEM(acts.shape, acts.dtype),
            pltpu.VMEM(grads.shape, grads.dtype),
            pltpu.VMEM(in_w.shape, in_w.dtype),
            pltpu.VMEM(out_w.shape, out_w.dtype),
            pltpu.SemaphoreType.DMA((ff // step + 1, 2)),
        ],
        compiler_params=pltpu.CompilerParams(vmem_limit_bytes=VMEM_BYTES),
        name="project",
    )(acts, grads, in_w, out_w)
    return pl.pallas_call(
        mark_kernel,
        in_specs=[VMEM, VMEM],
        out_specs=VMEM,
        out_shape=jax.ShapeDtypeStruct(
            (tokens, width + round_up(queries, LANES)), jnp.bfloat16
        ),
        compiler_params=pltpu.CompilerParams(vmem_limit_bytes=2 << 20),
        cost_estimate=pl.CostEstimate(
            flops=10**11, bytes_accessed=10**8, transcendentals=0
        ),
        name="mark",
    )(raw, ids)


def precond_kernel(tok, inverse, out, out_t, member_t, acc, *, kin, kout, per, queries):
    out_t[...] = tok[:, kin : kin + kout].astype(jnp.float32).T.astype(jnp.bfloat16)
    member_t[...] = (
        tok[:, kin + kout :].astype(jnp.float32).T[:queries].astype(jnp.bfloat16)
    )
    acc[...] = jnp.zeros_like(acc)

    def step(s):
        o = out_t[pl.ds(pl.multiple_of(s * per, per), per), :]
        weighted = (o[:, None, :] * member_t[...][None, :, :]).reshape(per * queries, o.shape[1])
        g = jnp.dot(weighted, tok[:, :kin], preferred_element_type=jnp.float32)
        g = g.astype(jnp.bfloat16)
        g = jnp.concatenate([g[k * queries : (k + 1) * queries] for k in range(per)], axis=1)
        block = inverse[:, pl.ds(pl.multiple_of(s * per * kin, per * kin), per * kin)]
        acc[...] += lax.dot_general(g, block, NT, preferred_element_type=jnp.float32)

    pl.loop(0, kout // per)(step)
    out[...] = acc[...].astype(jnp.bfloat16)


def precondition(tok, inverse, kin, kout, queries):
    rows, coords = inverse.shape
    tokens = tok.shape[0]
    per = chunk_of(kout, 16)
    return pl.pallas_call(
        functools.partial(precond_kernel, kin=kin, kout=kout, per=per, queries=queries),
        in_specs=[VMEM, VMEM],
        out_specs=VMEM,
        out_shape=jax.ShapeDtypeStruct((queries, rows), jnp.bfloat16),
        scratch_shapes=[
            pltpu.VMEM((kout, tokens), jnp.bfloat16),
            pltpu.VMEM((queries, tokens), jnp.bfloat16),
            pltpu.VMEM((queries, rows), jnp.float32),
        ],
        compiler_params=pltpu.CompilerParams(vmem_limit_bytes=16 << 20),
        cost_estimate=pl.CostEstimate(
            flops=2 * queries * rows * coords,
            bytes_accessed=2 * rows * coords,
            transcendentals=0,
        ),
        name="precondition",
    )(tok, inverse)


def score_kernel(near, far, stored, ids, out, *, masks, axis):
    me = lax.axis_index(axis)
    rows = near.shape[2]
    scores = jnp.zeros((stored.shape[0], near.shape[1]), jnp.float32)
    half = len(masks) // 2
    for n, mask in enumerate(masks):
        block = near[n] if n < half else far[n - half]
        start = pl.multiple_of((me ^ mask) * rows, rows)
        scores += lax.dot_general(
            stored[:, pl.ds(start, rows)], block, NT, preferred_element_type=jnp.float32
        )
    example = lax.broadcasted_iota(jnp.int32, (out.shape[0], ids.shape[1]), 0)
    member = jnp.where(example == ids[...], 1.0, 0.0)
    out[...] = jnp.dot(
        member, scores, precision=lax.Precision.HIGHEST, preferred_element_type=jnp.float32
    )


def score(near, far, stored, ids, masks, queries):
    return pl.pallas_call(
        functools.partial(score_kernel, masks=masks, axis="rows"),
        in_specs=[VMEM] * 4,
        out_specs=VMEM,
        out_shape=jax.ShapeDtypeStruct((EX_DEV, queries), jnp.float32),
        compiler_params=pltpu.CompilerParams(vmem_limit_bytes=8 << 20),
        name="score",
    )(near, far, stored, ids)


def stages_of(n):
    bits = []
    bit = n // 2
    while bit:
        bits.append(bit)
        bit //= 2
    return bits


def swap(x, bit, n):
    return lax.ppermute(x, "rows", [(i, i ^ bit) for i in range(n)])


def on_device(
    in_acts, out_grads, in_projection, out_projection, inverse, stored_rows, query_ids, example_ids
):
    n = lax.axis_size("rows")
    bits = stages_of(n)
    queries = QRY_DEV * n
    kin, kout = in_projection.shape[0], out_projection.shape[0]
    tok = project(
        in_acts, out_grads, in_projection, out_projection, query_ids[None, :], queries
    )
    for bit in bits:
        tok = jnp.concatenate([tok, swap(tok, bit, n)], axis=0)
    near = precondition(tok, inverse, kin, kout, queries)[None]
    masks = [0]
    for bit in bits:
        masks += [m ^ bit for m in masks]
        far = swap(near, bit, n)
        if bit != bits[-1]:
            near = jnp.concatenate([near, far], axis=0)
    return score(near, far, stored_rows, example_ids, masks, queries)


def solution(mesh):
    placed = (
        P(("groups", "rows"), None),
        P(("groups", "rows"), None),
        P(),
        P(),
        P("rows", None),
        P(("groups", "rows"), None),
        P(("groups", "rows")),
        P(("groups", "rows"), None),
    )
    return jax.shard_map(
        on_device,
        mesh=mesh,
        in_specs=placed,
        out_specs=P(("groups", "rows"), None),
        check_vma=False,
    )
```

```python
import functools

import jax
import jax.numpy as jnp
from jax import lax
from jax.experimental import pallas as pl
from jax.experimental.pallas import tpu as pltpu
from jax.sharding import PartitionSpec as P

LANES = 128
QRY_DEV = 1
EX_DEV = 16
NT = (((1,), (1,)), ((), ()))
VMEM = pl.BlockSpec(memory_space=pltpu.VMEM)
ANY = pl.BlockSpec(memory_space=pl.ANY)
VMEM_BYTES = 67_043_328 - (3 << 15)


def chunk_of(total, most):
    size = most
    while total % size:
        size //= 2
    return size


def round_up(n, m):
    return -(-n // m) * m


def taper(total, parts):
    tiles = total // LANES
    sizes = []
    for left in range(parts, 0, -1):
        size = tiles if left == 1 else -(-2 * tiles // (left + 1))
        sizes.append(size * LANES)
        tiles -= size
    return [size for size in sizes if size]


def project_kernel(acts, grads, in_w, out_w, raw, acts_v, grads_v, in_v, out_v, sem, *, sizes):
    pieces = [(grads, grads_v, out_w, out_v, 0, grads.shape[1])]
    for n, size in enumerate(sizes):
        pieces.append((acts, acts_v, in_w, in_v, sum(sizes[:n]), size))
    copies = []
    for n, (x, x_v, w, w_v, k, size) in enumerate(pieces):
        cols = pl.ds(k, size)
        copies.append(
            (
                pltpu.make_async_copy(x.at[:, cols], x_v.at[:, cols], sem.at[n, 0]),
                pltpu.make_async_copy(w.at[:, cols], w_v.at[:, cols], sem.at[n, 1]),
            )
        )
    for pair in copies:
        for copy in pair:
            copy.start()
    kin = in_w.shape[0]
    total = None
    for n, (x, x_v, w, w_v, k, size) in enumerate(pieces):
        for copy in copies[n]:
            copy.wait()
        part = lax.dot_general(
            x_v[:, k : k + size], w_v[:, k : k + size], NT, preferred_element_type=jnp.float32
        )
        if n == 0:
            raw[:, kin:] = part.astype(jnp.bfloat16)
        else:
            total = part if total is None else total + part
    raw[:, :kin] = total.astype(jnp.bfloat16)


def mark_kernel(raw, ids, tok):
    tokens, done = raw.shape
    row = lax.broadcasted_iota(jnp.int32, (tokens, tokens), 0)
    col = lax.broadcasted_iota(jnp.int32, (tokens, tokens), 1)
    mine = jnp.sum(jnp.where(row == col, ids[...], 0), axis=1, keepdims=True)
    query = lax.broadcasted_iota(jnp.int32, (tokens, tok.shape[1] - done), 1)
    tok[:, :done] = raw[...]
    tok[:, done:] = jnp.where(query == mine, 1.0, 0.0).astype(jnp.bfloat16)


def project(acts, grads, in_w, out_w, ids, queries):
    tokens, ff = acts.shape
    sizes = taper(ff, 5)
    width = in_w.shape[0] + out_w.shape[0]
    raw = pl.pallas_call(
        functools.partial(project_kernel, sizes=sizes),
        in_specs=[ANY] * 4,
        out_specs=VMEM,
        out_shape=jax.ShapeDtypeStruct((tokens, width), jnp.bfloat16),
        scratch_shapes=[
            pltpu.VMEM(acts.shape, acts.dtype),
            pltpu.VMEM(grads.shape, grads.dtype),
            pltpu.VMEM(in_w.shape, in_w.dtype),
            pltpu.VMEM(out_w.shape, out_w.dtype),
            pltpu.SemaphoreType.DMA((len(sizes) + 1, 2)),
        ],
        compiler_params=pltpu.CompilerParams(vmem_limit_bytes=VMEM_BYTES),
        name="project",
    )(acts, grads, in_w, out_w)
    return pl.pallas_call(
        mark_kernel,
        in_specs=[VMEM, VMEM],
        out_specs=VMEM,
        out_shape=jax.ShapeDtypeStruct(
            (tokens, width + round_up(queries, LANES)), jnp.bfloat16
        ),
        compiler_params=pltpu.CompilerParams(vmem_limit_bytes=2 << 20),
        cost_estimate=pl.CostEstimate(
            flops=10**11, bytes_accessed=10**8, transcendentals=0
        ),
        name="mark",
    )(raw, ids)


def precond_kernel(tok, inverse, out, out_t, member_t, *acc, kin, kout, per, fold, queries):
    out_t[...] = tok[:, kin : kin + kout].astype(jnp.float32).T.astype(jnp.bfloat16)
    member_t[...] = (
        tok[:, kin + kout :].astype(jnp.float32).T[:queries].astype(jnp.bfloat16)
    )

    def grads(first):
        o = out_t[pl.ds(first, per), :]
        weighted = (o[:, None, :] * member_t[...][None, :, :]).reshape(per * queries, o.shape[1])
        g = jnp.dot(weighted, tok[:, :kin], preferred_element_type=jnp.float32)
        g = g.astype(jnp.bfloat16)
        return [g[k * queries : (k + 1) * queries] for k in range(per)]

    def product(first):
        g = []
        for n in range(fold):
            g += grads(first + n * per)
        start = first * kin if isinstance(first, int) else pl.multiple_of(first * kin, kin)
        block = inverse[:, pl.ds(start, fold * per * kin)]
        return lax.dot_general(
            jnp.concatenate(g, axis=1), block, NT, preferred_element_type=jnp.float32
        )

    if not acc:
        out[...] = product(0).astype(jnp.bfloat16)
        return
    total = acc[0]
    total[...] = jnp.zeros_like(total)

    def step(s):
        total[...] += product(s * (fold * per))

    pl.loop(0, kout // (fold * per))(step)
    out[...] = total[...].astype(jnp.bfloat16)


def precondition(tok, inverse, kin, kout, queries):
    rows, coords = inverse.shape
    tokens = tok.shape[0]
    per = chunk_of(kout, max(8, (1 << 16) // (queries * tokens)))
    fold = chunk_of(kout // per, max(1, (1 << 18) // (per * queries * tokens) * 2))
    scratch = [
        pltpu.VMEM((kout, tokens), jnp.bfloat16),
        pltpu.VMEM((queries, tokens), jnp.bfloat16),
    ]
    if fold * per < kout:
        scratch.append(pltpu.VMEM((queries, rows), jnp.float32))
    return pl.pallas_call(
        functools.partial(
            precond_kernel, kin=kin, kout=kout, per=per, fold=fold, queries=queries
        ),
        in_specs=[VMEM, VMEM],
        out_specs=VMEM,
        out_shape=jax.ShapeDtypeStruct((queries, rows), jnp.bfloat16),
        scratch_shapes=scratch,
        compiler_params=pltpu.CompilerParams(vmem_limit_bytes=16 << 20),
        cost_estimate=pl.CostEstimate(
            flops=2 * queries * rows * coords,
            bytes_accessed=2 * rows * coords,
            transcendentals=0,
        ),
        name="precondition",
    )(tok, inverse)


def block_scores(blocks, stored, masks, axis):
    me = lax.axis_index(axis)
    rows = blocks.shape[2]
    scores = jnp.zeros((stored.shape[0], blocks.shape[1]), jnp.float32)
    for n, mask in enumerate(masks):
        start = pl.multiple_of((me ^ mask) * rows, rows)
        scores += lax.dot_general(
            stored[:, pl.ds(start, rows)], blocks[n], NT, preferred_element_type=jnp.float32
        )
    return scores


def near_kernel(near, stored, part, *, masks, axis):
    part[...] = block_scores(near, stored, masks, axis)


def far_kernel(far, part, stored, ids, out, *, masks, axis):
    scores = part[...] + block_scores(far, stored, masks, axis)
    example = lax.broadcasted_iota(jnp.int32, (out.shape[0], ids.shape[1]), 0)
    member = jnp.where(example == ids[...], 1.0, 0.0)
    out[...] = jnp.dot(
        member, scores, precision=lax.Precision.HIGHEST, preferred_element_type=jnp.float32
    )


def score_cost(stored, queries):
    return pl.CostEstimate(
        flops=stored.size * queries, bytes_accessed=stored.size, transcendentals=0
    )


def score_near(near, stored, masks, queries):
    return pl.pallas_call(
        functools.partial(near_kernel, masks=masks, axis="rows"),
        in_specs=[VMEM] * 2,
        out_specs=VMEM,
        out_shape=jax.ShapeDtypeStruct((stored.shape[0], queries), jnp.float32),
        compiler_params=pltpu.CompilerParams(vmem_limit_bytes=8 << 20),
        cost_estimate=score_cost(stored, queries),
        name="score_near",
    )(near, stored)


def score_far(far, part, stored, ids, masks, queries):
    return pl.pallas_call(
        functools.partial(far_kernel, masks=masks, axis="rows"),
        in_specs=[VMEM] * 4,
        out_specs=VMEM,
        out_shape=jax.ShapeDtypeStruct((EX_DEV, queries), jnp.float32),
        compiler_params=pltpu.CompilerParams(vmem_limit_bytes=8 << 20),
        cost_estimate=score_cost(stored, queries),
        name="score_far",
    )(far, part, stored, ids)


def stages_of(n, crossed):
    masks = []
    bit = n // 2
    while bit:
        masks.append(bit | 1 if len(masks) < crossed else bit)
        bit //= 2
    return masks


def swap(x, mask, n):
    return lax.ppermute(x, "rows", [(i, i ^ mask) for i in range(n)])


def on_device(
    in_acts, out_grads, in_projection, out_projection, inverse, stored_rows, query_ids, example_ids
):
    n = lax.axis_size("rows")
    queries = QRY_DEV * n
    kin, kout = in_projection.shape[0], out_projection.shape[0]
    tok = project(
        in_acts, out_grads, in_projection, out_projection, query_ids[None, :], queries
    )
    for mask in stages_of(n, n):
        tok = jnp.concatenate([tok, swap(tok, mask, n)], axis=0)
    near = precondition(tok, inverse, kin, kout, queries)[None]
    held = [0]
    *stages, last = stages_of(n, 1)
    for mask in stages:
        held += [m ^ mask for m in held]
        near = jnp.concatenate([near, swap(near, mask, n)], axis=0)
    far = swap(near, last, n)
    part = score_near(near, stored_rows, held, queries)
    return score_far(far, part, stored_rows, example_ids, [m ^ last for m in held], queries)


def solution(mesh):
    placed = (
        P(("groups", "rows"), None),
        P(("groups", "rows"), None),
        P(),
        P(),
        P("rows", None),
        P(("groups", "rows"), None),
        P(("groups", "rows")),
        P(("groups", "rows"), None),
    )
    return jax.shard_map(
        on_device,
        mesh=mesh,
        in_specs=placed,
        out_specs=P(("groups", "rows"), None),
        check_vma=False,
    )
```

```python
import functools

import jax
import jax.numpy as jnp
from jax import lax
from jax.experimental import pallas as pl
from jax.experimental.pallas import tpu as pltpu
from jax.sharding import PartitionSpec as P

LANES = 128
QRY_DEV = 1
EX_DEV = 16
NT = (((1,), (1,)), ((), ()))
VMEM = pl.BlockSpec(memory_space=pltpu.VMEM)
ANY = pl.BlockSpec(memory_space=pl.ANY)
PROJECT_VMEM = 56_543_328


def chunk_of(total, most):
    size = most
    while total % size:
        size //= 2
    return size


def round_up(n, m):
    return -(-n // m) * m


def taper(total, parts):
    tiles = total // LANES
    sizes = []
    for left in range(parts, 0, -1):
        size = tiles if left == 1 else -(-2 * tiles // (left + 1))
        sizes.append(size * LANES)
        tiles -= size
    return [size for size in sizes if size]


def project_kernel(acts, grads, in_w, out_w, raw, acts_v, grads_v, in_v, out_v, sem, *, sizes):
    pieces = [(grads, grads_v, out_w, out_v, 0, grads.shape[1])]
    for n, size in enumerate(sizes):
        pieces.append((acts, acts_v, in_w, in_v, sum(sizes[:n]), size))
    copies = []
    for n, (x, x_v, w, w_v, k, size) in enumerate(pieces):
        cols = pl.ds(k, size)
        copies.append(
            (
                pltpu.make_async_copy(x.at[:, cols], x_v.at[:, cols], sem.at[n, 0]),
                pltpu.make_async_copy(w.at[:, cols], w_v.at[:, cols], sem.at[n, 1]),
            )
        )
    for pair in copies:
        for copy in pair:
            copy.start()
    kin = in_w.shape[0]
    total = None
    for n, (x, x_v, w, w_v, k, size) in enumerate(pieces):
        for copy in copies[n]:
            copy.wait()
        part = lax.dot_general(
            x_v[:, k : k + size], w_v[:, k : k + size], NT, preferred_element_type=jnp.float32
        )
        if n == 0:
            raw[:, kin:] = part.astype(jnp.bfloat16)
        else:
            total = part if total is None else total + part
    raw[:, :kin] = total.astype(jnp.bfloat16)


def mark_kernel(raw, ids, tok):
    tokens, done = raw.shape
    row = lax.broadcasted_iota(jnp.int32, (tokens, tokens), 0)
    col = lax.broadcasted_iota(jnp.int32, (tokens, tokens), 1)
    mine = jnp.sum(jnp.where(row == col, ids[...], 0), axis=1, keepdims=True)
    query = lax.broadcasted_iota(jnp.int32, (tokens, tok.shape[1] - done), 1)
    tok[:, :done] = raw[...]
    tok[:, done:] = jnp.where(query == mine, 1.0, 0.0).astype(jnp.bfloat16)


def project(acts, grads, in_w, out_w, ids, queries):
    tokens, ff = acts.shape
    sizes = taper(ff, 5)
    width = in_w.shape[0] + out_w.shape[0]
    raw = pl.pallas_call(
        functools.partial(project_kernel, sizes=sizes),
        in_specs=[ANY] * 4,
        out_specs=VMEM,
        out_shape=jax.ShapeDtypeStruct((tokens, width), jnp.bfloat16),
        scratch_shapes=[
            pltpu.VMEM(acts.shape, acts.dtype),
            pltpu.VMEM(grads.shape, grads.dtype),
            pltpu.VMEM(in_w.shape, in_w.dtype),
            pltpu.VMEM(out_w.shape, out_w.dtype),
            pltpu.SemaphoreType.DMA((len(sizes) + 1, 2)),
        ],
        compiler_params=pltpu.CompilerParams(vmem_limit_bytes=PROJECT_VMEM),
        name="project",
    )(acts, grads, in_w, out_w)
    return pl.pallas_call(
        mark_kernel,
        in_specs=[VMEM, VMEM],
        out_specs=VMEM,
        out_shape=jax.ShapeDtypeStruct(
            (tokens, width + round_up(queries, LANES)), jnp.bfloat16
        ),
        compiler_params=pltpu.CompilerParams(vmem_limit_bytes=2 << 20),
        cost_estimate=pl.CostEstimate(
            flops=10**11, bytes_accessed=10**8, transcendentals=0
        ),
        name="mark",
    )(raw, ids)


def precond_kernel(tok, inverse, out, out_t, member_t, *acc, kin, kout, per, fold, queries):
    out_t[...] = tok[:, kin : kin + kout].astype(jnp.float32).T.astype(jnp.bfloat16)
    member_t[...] = (
        tok[:, kin + kout :].astype(jnp.float32).T[:queries].astype(jnp.bfloat16)
    )

    def grads(first):
        o = out_t[pl.ds(first, per), :]
        weighted = (o[:, None, :] * member_t[...][None, :, :]).reshape(per * queries, o.shape[1])
        g = jnp.dot(weighted, tok[:, :kin], preferred_element_type=jnp.float32)
        g = g.astype(jnp.bfloat16)
        return [g[k * queries : (k + 1) * queries] for k in range(per)]

    def product(first):
        g = []
        for n in range(fold):
            g += grads(first + n * per)
        start = first * kin if isinstance(first, int) else pl.multiple_of(first * kin, kin)
        block = inverse[:, pl.ds(start, fold * per * kin)]
        return lax.dot_general(
            jnp.concatenate(g, axis=1), block, NT, preferred_element_type=jnp.float32
        )

    if not acc:
        out[...] = product(0).astype(jnp.bfloat16)
        return
    total = acc[0]
    total[...] = jnp.zeros_like(total)

    def step(s):
        total[...] += product(s * (fold * per))

    pl.loop(0, kout // (fold * per))(step)
    out[...] = total[...].astype(jnp.bfloat16)


def precondition(tok, inverse, kin, kout, queries):
    rows, coords = inverse.shape
    tokens = tok.shape[0]
    per = chunk_of(kout, max(8, (1 << 16) // (queries * tokens)))
    fold = chunk_of(kout // per, max(1, (1 << 18) // (per * queries * tokens) * 2))
    scratch = [
        pltpu.VMEM((kout, tokens), jnp.bfloat16),
        pltpu.VMEM((queries, tokens), jnp.bfloat16),
    ]
    if fold * per < kout:
        scratch.append(pltpu.VMEM((queries, rows), jnp.float32))
    return pl.pallas_call(
        functools.partial(
            precond_kernel, kin=kin, kout=kout, per=per, fold=fold, queries=queries
        ),
        in_specs=[VMEM, VMEM],
        out_specs=VMEM,
        out_shape=jax.ShapeDtypeStruct((queries, rows), jnp.bfloat16),
        scratch_shapes=scratch,
        compiler_params=pltpu.CompilerParams(vmem_limit_bytes=16 << 20),
        cost_estimate=pl.CostEstimate(
            flops=2 * queries * rows * coords,
            bytes_accessed=2 * rows * coords,
            transcendentals=0,
        ),
        name="precondition",
    )(tok, inverse)


def block_scores(blocks, stored, masks, axis):
    me = lax.axis_index(axis)
    rows = blocks.shape[2]
    scores = jnp.zeros((stored.shape[0], blocks.shape[1]), jnp.float32)
    for n, mask in enumerate(masks):
        start = pl.multiple_of((me ^ mask) * rows, rows)
        scores += lax.dot_general(
            stored[:, pl.ds(start, rows)], blocks[n], NT, preferred_element_type=jnp.float32
        )
    return scores


def near_kernel(near, stored, part, *, masks, axis):
    part[...] = block_scores(near, stored, masks, axis)


def far_kernel(far, part, stored, ids, out, *, masks, axis):
    scores = part[...] + block_scores(far, stored, masks, axis)
    example = lax.broadcasted_iota(jnp.int32, (out.shape[0], ids.shape[1]), 0)
    member = jnp.where(example == ids[...], 1.0, 0.0)
    out[...] = jnp.dot(
        member, scores, precision=lax.Precision.HIGHEST, preferred_element_type=jnp.float32
    )


def score_cost(stored, queries):
    return pl.CostEstimate(
        flops=stored.size * queries, bytes_accessed=stored.size, transcendentals=0
    )


def score_near(near, stored, masks, queries):
    return pl.pallas_call(
        functools.partial(near_kernel, masks=masks, axis="rows"),
        in_specs=[VMEM] * 2,
        out_specs=VMEM,
        out_shape=jax.ShapeDtypeStruct((stored.shape[0], queries), jnp.float32),
        compiler_params=pltpu.CompilerParams(vmem_limit_bytes=8 << 20),
        cost_estimate=score_cost(stored, queries),
        name="score_near",
    )(near, stored)


def score_far(far, part, stored, ids, masks, queries):
    return pl.pallas_call(
        functools.partial(far_kernel, masks=masks, axis="rows"),
        in_specs=[VMEM] * 4,
        out_specs=VMEM,
        out_shape=jax.ShapeDtypeStruct((EX_DEV, queries), jnp.float32),
        compiler_params=pltpu.CompilerParams(vmem_limit_bytes=8 << 20),
        cost_estimate=score_cost(stored, queries),
        name="score_far",
    )(far, part, stored, ids)


def rounds_of(n):
    bits = []
    bit = n // 2
    while bit > 1:
        bits.append(bit)
        bit //= 2
    rounds = [[bits[0] | 1]] if bits else []
    for k in range(1, len(bits), 2):
        pair = bits[k : k + 2]
        rounds.append([m | 1 for m in ([sum(pair)] if len(pair) == 2 else []) + pair])
    return rounds + [[1]]


def swap(x, mask, n):
    return lax.ppermute(x, "rows", [(i, i ^ mask) for i in range(n)])


def spread(x, held, masks, n):
    pieces = [x] + [swap(x, mask, n) for mask in masks]
    held = held + [h ^ mask for mask in masks for h in held]
    return jnp.concatenate(pieces, axis=0), held


def on_device(
    in_acts, out_grads, in_projection, out_projection, inverse, stored_rows, query_ids, example_ids
):
    n = lax.axis_size("rows")
    queries = QRY_DEV * n
    kin, kout = in_projection.shape[0], out_projection.shape[0]
    tok = project(
        in_acts, out_grads, in_projection, out_projection, query_ids[None, :], queries
    )
    *rounds, (last,) = rounds_of(n)
    for masks in rounds:
        tok, _ = spread(tok, [0], masks, n)
    tok, _ = spread(tok, [0], [last], n)
    near, held = precondition(tok, inverse, kin, kout, queries)[None], [0]
    for masks in rounds:
        near, held = spread(near, held, masks, n)
    far = swap(near, last, n)
    part = score_near(near, stored_rows, held, queries)
    return score_far(far, part, stored_rows, example_ids, [h ^ last for h in held], queries)


def solution(mesh):
    placed = (
        P(("groups", "rows"), None),
        P(("groups", "rows"), None),
        P(),
        P(),
        P("rows", None),
        P(("groups", "rows"), None),
        P(("groups", "rows")),
        P(("groups", "rows"), None),
    )
    return jax.shard_map(
        on_device,
        mesh=mesh,
        in_specs=placed,
        out_specs=P(("groups", "rows"), None),
        check_vma=False,
    )
```

```python
import functools

import jax
import jax.numpy as jnp
from jax import lax
from jax.experimental import pallas as pl
from jax.experimental.pallas import tpu as pltpu
from jax.sharding import PartitionSpec as P

LANES = 128
QRY_DEV = 1
EX_DEV = 16
NT = (((1,), (1,)), ((), ()))
VMEM = pl.BlockSpec(memory_space=pltpu.VMEM)
ANY = pl.BlockSpec(memory_space=pl.ANY)
PROJECT_VMEM = 56_543_328


def chunk_of(total, most):
    size = most
    while total % size:
        size //= 2
    return size


def round_up(n, m):
    return -(-n // m) * m


def portions(total, weights):
    unit = 2 * LANES
    cuts = [total * sum(weights[:k]) // sum(weights) // unit * unit for k in range(len(weights))]
    cuts.append(total)
    return [(lo, hi - lo) for lo, hi in zip(cuts, cuts[1:])]


def project_kernel(acts, grads, in_w, out_w, raw, acts_v, grads_v, in_v, out_v, sem, *, steps):
    copies = []
    for n, (own, other) in enumerate(steps):
        parts = ((grads, grads_v, other), (out_w, out_v, other), (acts, acts_v, own), (in_w, in_v, own))
        copies.append(
            [
                pltpu.make_async_copy(
                    src.at[:, pl.ds(start, size)], dst.at[:, pl.ds(start, size)], sem.at[n, k]
                )
                for k, (src, dst, (start, size)) in enumerate(parts)
            ]
        )
    for step in copies:
        for copy in step:
            copy.start()

    def product(x, w, start, size):
        return lax.dot_general(
            x[:, start : start + size],
            w[:, start : start + size],
            NT,
            preferred_element_type=jnp.float32,
        )

    kin = in_w.shape[0]
    in_sum, out_sum = [], []
    for n, ((start, size), other) in enumerate(steps):
        for copy in copies[n]:
            copy.wait()
        half = size // 2
        in_sum += [
            product(acts_v, in_v, start, half),
            product(acts_v, in_v, start + half, size - half),
        ]
        out_sum.append(product(grads_v, out_v, *other))
    raw[:, :kin] = sum(in_sum[1:], in_sum[0]).astype(jnp.bfloat16)
    raw[:, kin:] = sum(out_sum[1:], out_sum[0]).astype(jnp.bfloat16)


def mark_kernel(raw, ids, tok):
    tokens, done = raw.shape
    row = lax.broadcasted_iota(jnp.int32, (tokens, tokens), 0)
    col = lax.broadcasted_iota(jnp.int32, (tokens, tokens), 1)
    mine = jnp.sum(jnp.where(row == col, ids[...], 0), axis=1, keepdims=True)
    query = lax.broadcasted_iota(jnp.int32, (tokens, tok.shape[1] - done), 1)
    tok[:, :done] = raw[...]
    tok[:, done:] = jnp.where(query == mine, 1.0, 0.0).astype(jnp.bfloat16)


def project(acts, grads, in_w, out_w, ids, queries):
    tokens, ff = acts.shape
    steps = list(zip(portions(ff, (2, 2, 2, 1)), portions(grads.shape[1], (1, 1, 1, 1))))
    width = in_w.shape[0] + out_w.shape[0]
    raw = pl.pallas_call(
        functools.partial(project_kernel, steps=steps),
        in_specs=[ANY] * 4,
        out_specs=VMEM,
        out_shape=jax.ShapeDtypeStruct((tokens, width), jnp.bfloat16),
        scratch_shapes=[
            pltpu.VMEM(acts.shape, acts.dtype),
            pltpu.VMEM(grads.shape, grads.dtype),
            pltpu.VMEM(in_w.shape, in_w.dtype),
            pltpu.VMEM(out_w.shape, out_w.dtype),
            pltpu.SemaphoreType.DMA((len(steps), 4)),
        ],
        compiler_params=pltpu.CompilerParams(vmem_limit_bytes=PROJECT_VMEM),
        name="project",
    )(acts, grads, in_w, out_w)
    return pl.pallas_call(
        mark_kernel,
        in_specs=[VMEM, VMEM],
        out_specs=VMEM,
        out_shape=jax.ShapeDtypeStruct(
            (tokens, width + round_up(queries, LANES)), jnp.bfloat16
        ),
        compiler_params=pltpu.CompilerParams(vmem_limit_bytes=2 << 20),
        cost_estimate=pl.CostEstimate(
            flops=10**11, bytes_accessed=10**8, transcendentals=0
        ),
        name="mark",
    )(raw, ids)


def precond_kernel(tok, inverse, out, out_t, member_t, *acc, kin, kout, per, fold, queries):
    out_t[...] = tok[:, kin : kin + kout].astype(jnp.float32).T.astype(jnp.bfloat16)
    member_t[...] = (
        tok[:, kin + kout :].astype(jnp.float32).T[:queries].astype(jnp.bfloat16)
    )

    def grads(first):
        o = out_t[pl.ds(first, per), :]
        weighted = (o[:, None, :] * member_t[...][None, :, :]).reshape(per * queries, o.shape[1])
        g = jnp.dot(weighted, tok[:, :kin], preferred_element_type=jnp.float32)
        g = g.astype(jnp.bfloat16)
        return [g[k * queries : (k + 1) * queries] for k in range(per)]

    def product(first):
        g = []
        for n in range(fold):
            g += grads(first + n * per)
        start = first * kin if isinstance(first, int) else pl.multiple_of(first * kin, kin)
        block = inverse[:, pl.ds(start, fold * per * kin)]
        return lax.dot_general(
            jnp.concatenate(g, axis=1), block, NT, preferred_element_type=jnp.float32
        )

    if not acc:
        out[...] = product(0).astype(jnp.bfloat16)
        return
    total = acc[0]
    total[...] = jnp.zeros_like(total)

    def step(s):
        total[...] += product(s * (fold * per))

    pl.loop(0, kout // (fold * per))(step)
    out[...] = total[...].astype(jnp.bfloat16)


def precondition(tok, inverse, kin, kout, queries):
    rows, coords = inverse.shape
    tokens = tok.shape[0]
    per = chunk_of(kout, max(8, (1 << 16) // (queries * tokens)))
    fold = chunk_of(kout // per, max(1, (1 << 18) // (per * queries * tokens) * 2))
    scratch = [
        pltpu.VMEM((kout, tokens), jnp.bfloat16),
        pltpu.VMEM((queries, tokens), jnp.bfloat16),
    ]
    if fold * per < kout:
        scratch.append(pltpu.VMEM((queries, rows), jnp.float32))
    return pl.pallas_call(
        functools.partial(
            precond_kernel, kin=kin, kout=kout, per=per, fold=fold, queries=queries
        ),
        in_specs=[VMEM, VMEM],
        out_specs=VMEM,
        out_shape=jax.ShapeDtypeStruct((queries, rows), jnp.bfloat16),
        scratch_shapes=scratch,
        compiler_params=pltpu.CompilerParams(vmem_limit_bytes=16 << 20),
        cost_estimate=pl.CostEstimate(
            flops=2 * queries * rows * coords,
            bytes_accessed=2 * rows * coords,
            transcendentals=0,
        ),
        name="precondition",
    )(tok, inverse)


def block_scores(blocks, stored, masks, axis):
    me = lax.axis_index(axis)
    rows = blocks.shape[2]
    scores = jnp.zeros((stored.shape[0], blocks.shape[1]), jnp.float32)
    for n, mask in enumerate(masks):
        start = pl.multiple_of((me ^ mask) * rows, rows)
        scores += lax.dot_general(
            stored[:, pl.ds(start, rows)], blocks[n], NT, preferred_element_type=jnp.float32
        )
    return scores


def near_kernel(near, stored, part, *, masks, axis):
    part[...] = block_scores(near, stored, masks, axis)


def far_kernel(far, part, stored, ids, out, *, masks, axis):
    scores = part[...] + block_scores(far, stored, masks, axis)
    example = lax.broadcasted_iota(jnp.int32, (out.shape[0], ids.shape[1]), 0)
    member = jnp.where(example == ids[...], 1.0, 0.0)
    out[...] = jnp.dot(
        member, scores, precision=lax.Precision.HIGHEST, preferred_element_type=jnp.float32
    )


def score_cost(stored, queries):
    return pl.CostEstimate(
        flops=stored.size * queries, bytes_accessed=stored.size, transcendentals=0
    )


def score_near(near, stored, masks, queries):
    return pl.pallas_call(
        functools.partial(near_kernel, masks=masks, axis="rows"),
        in_specs=[VMEM] * 2,
        out_specs=VMEM,
        out_shape=jax.ShapeDtypeStruct((stored.shape[0], queries), jnp.float32),
        compiler_params=pltpu.CompilerParams(vmem_limit_bytes=8 << 20),
        cost_estimate=score_cost(stored, queries),
        name="score_near",
    )(near, stored)


def score_far(far, part, stored, ids, masks, queries):
    return pl.pallas_call(
        functools.partial(far_kernel, masks=masks, axis="rows"),
        in_specs=[VMEM] * 4,
        out_specs=VMEM,
        out_shape=jax.ShapeDtypeStruct((EX_DEV, queries), jnp.float32),
        compiler_params=pltpu.CompilerParams(vmem_limit_bytes=8 << 20),
        cost_estimate=score_cost(stored, queries),
        name="score_far",
    )(far, part, stored, ids)


def rounds_of(n):
    bits = []
    bit = n // 2
    while bit > 1:
        bits.append(bit)
        bit //= 2
    rounds = [[bits[0] | 1]] if bits else []
    for k in range(1, len(bits), 2):
        pair = bits[k : k + 2]
        rounds.append([m | 1 for m in ([sum(pair)] if len(pair) == 2 else []) + pair])
    return rounds + [[1]]


def swap(x, mask, n):
    return lax.ppermute(x, "rows", [(i, i ^ mask) for i in range(n)])


def spread(x, held, masks, n):
    pieces = [x] + [swap(x, mask, n) for mask in masks]
    held = held + [h ^ mask for mask in masks for h in held]
    return jnp.concatenate(pieces, axis=0), held


def on_device(
    in_acts, out_grads, in_projection, out_projection, inverse, stored_rows, query_ids, example_ids
):
    n = lax.axis_size("rows")
    queries = QRY_DEV * n
    kin, kout = in_projection.shape[0], out_projection.shape[0]
    tok = project(
        in_acts, out_grads, in_projection, out_projection, query_ids[None, :], queries
    )
    *rounds, (last,) = rounds_of(n)
    for masks in rounds:
        tok, _ = spread(tok, [0], masks, n)
    tok, _ = spread(tok, [0], [last], n)
    near, held = precondition(tok, inverse, kin, kout, queries)[None], [0]
    for masks in rounds:
        near, held = spread(near, held, masks, n)
    far = swap(near, last, n)
    part = score_near(near, stored_rows, held, queries)
    return score_far(far, part, stored_rows, example_ids, [h ^ last for h in held], queries)


def solution(mesh):
    placed = (
        P(("groups", "rows"), None),
        P(("groups", "rows"), None),
        P(),
        P(),
        P("rows", None),
        P(("groups", "rows"), None),
        P(("groups", "rows")),
        P(("groups", "rows"), None),
    )
    return jax.shard_map(
        on_device,
        mesh=mesh,
        in_specs=placed,
        out_specs=P(("groups", "rows"), None),
        check_vma=False,
    )
```

```python
import functools

import jax
import jax.numpy as jnp
from jax import lax
from jax.experimental import pallas as pl
from jax.experimental.pallas import tpu as pltpu
from jax.sharding import PartitionSpec as P

LANES = 128
QRY_DEV = 1
EX_DEV = 16
NT = (((1,), (1,)), ((), ()))
VMEM = pl.BlockSpec(memory_space=pltpu.VMEM)
ANY = pl.BlockSpec(memory_space=pl.ANY)
PROJECT_VMEM = 56_543_328


def chunk_of(total, most):
    size = most
    while total % size:
        size //= 2
    return size


def round_up(n, m):
    return -(-n // m) * m


def portions(total, weights):
    unit = 2 * LANES
    cuts = [total * sum(weights[:k]) // sum(weights) // unit * unit for k in range(len(weights))]
    cuts.append(total)
    return [(lo, hi - lo) for lo, hi in zip(cuts, cuts[1:])]


def project_kernel(acts, grads, in_w, out_w, raw, acts_v, grads_v, in_v, out_v, sem, *, steps):
    copies = []
    for n, (own, other) in enumerate(steps):
        parts = ((grads, grads_v, other), (out_w, out_v, other), (acts, acts_v, own), (in_w, in_v, own))
        copies.append(
            [
                pltpu.make_async_copy(
                    src.at[:, pl.ds(start, size)], dst.at[:, pl.ds(start, size)], sem.at[n, k]
                )
                for k, (src, dst, (start, size)) in enumerate(parts)
            ]
        )
    for step in copies:
        for copy in step:
            copy.start()

    def product(x, w, start, size):
        return lax.dot_general(
            x[:, start : start + size],
            w[:, start : start + size],
            NT,
            preferred_element_type=jnp.float32,
        )

    kin = in_w.shape[0]
    in_sum, out_sum = [], []
    for n, ((start, size), other) in enumerate(steps):
        for copy in copies[n]:
            copy.wait()
        half = size // 2
        in_sum += [
            product(acts_v, in_v, start, half),
            product(acts_v, in_v, start + half, size - half),
        ]
        out_sum.append(product(grads_v, out_v, *other))
    raw[:, :kin] = sum(in_sum[1:], in_sum[0]).astype(jnp.bfloat16)
    raw[:, kin:] = sum(out_sum[1:], out_sum[0]).astype(jnp.bfloat16)


def mark_kernel(raw, ids, tok):
    tokens, done = raw.shape
    row = lax.broadcasted_iota(jnp.int32, (tokens, tokens), 0)
    col = lax.broadcasted_iota(jnp.int32, (tokens, tokens), 1)
    mine = jnp.sum(jnp.where(row == col, ids[...], 0), axis=1, keepdims=True)
    query = lax.broadcasted_iota(jnp.int32, (tokens, tok.shape[1] - done), 1)
    tok[:, :done] = raw[...]
    tok[:, done:] = jnp.where(query == mine, 1.0, 0.0).astype(jnp.bfloat16)


def project(acts, grads, in_w, out_w, ids, queries):
    tokens, ff = acts.shape
    steps = list(zip(portions(ff, (2, 2, 2, 1)), portions(grads.shape[1], (1, 1, 1, 1))))
    width = in_w.shape[0] + out_w.shape[0]
    raw = pl.pallas_call(
        functools.partial(project_kernel, steps=steps),
        in_specs=[ANY] * 4,
        out_specs=VMEM,
        out_shape=jax.ShapeDtypeStruct((tokens, width), jnp.bfloat16),
        scratch_shapes=[
            pltpu.VMEM(acts.shape, acts.dtype),
            pltpu.VMEM(grads.shape, grads.dtype),
            pltpu.VMEM(in_w.shape, in_w.dtype),
            pltpu.VMEM(out_w.shape, out_w.dtype),
            pltpu.SemaphoreType.DMA((len(steps), 4)),
        ],
        compiler_params=pltpu.CompilerParams(vmem_limit_bytes=PROJECT_VMEM),
        name="project",
    )(acts, grads, in_w, out_w)
    return pl.pallas_call(
        mark_kernel,
        in_specs=[VMEM, VMEM],
        out_specs=VMEM,
        out_shape=jax.ShapeDtypeStruct(
            (tokens, width + round_up(queries, LANES)), jnp.bfloat16
        ),
        compiler_params=pltpu.CompilerParams(vmem_limit_bytes=2 << 20),
        cost_estimate=pl.CostEstimate(
            flops=10**11, bytes_accessed=10**8, transcendentals=0
        ),
        name="mark",
    )(raw, ids)


def precond_kernel(tok, inverse, out, out_t, member_t, *acc, kin, kout, per, fold, queries):
    out_t[...] = tok[:, kin : kin + kout].astype(jnp.float32).T.astype(jnp.bfloat16)
    member_t[...] = (
        tok[:, kin + kout :].astype(jnp.float32).T[:queries].astype(jnp.bfloat16)
    )

    def grads(first):
        o = out_t[pl.ds(first, per), :]
        weighted = (o[:, None, :] * member_t[...][None, :, :]).reshape(per * queries, o.shape[1])
        g = jnp.dot(weighted, tok[:, :kin], preferred_element_type=jnp.float32)
        g = g.astype(jnp.bfloat16)
        return [g[k * queries : (k + 1) * queries] for k in range(per)]

    def product(first):
        g = []
        for n in range(fold):
            g += grads(first + n * per)
        start = first * kin if isinstance(first, int) else pl.multiple_of(first * kin, kin)
        block = inverse[:, pl.ds(start, fold * per * kin)]
        return lax.dot_general(
            jnp.concatenate(g, axis=1), block, NT, preferred_element_type=jnp.float32
        )

    if not acc:
        out[...] = product(0).astype(jnp.bfloat16)
        return
    total = acc[0]
    total[...] = jnp.zeros_like(total)

    def step(s):
        total[...] += product(s * (fold * per))

    pl.loop(0, kout // (fold * per))(step)
    out[...] = total[...].astype(jnp.bfloat16)


def precondition(tok, inverse, kin, kout, queries):
    rows, coords = inverse.shape
    tokens = tok.shape[0]
    per = chunk_of(kout, max(8, (1 << 16) // (queries * tokens)))
    fold = chunk_of(kout // per, max(1, (1 << 18) // (per * queries * tokens) * 2))
    scratch = [
        pltpu.VMEM((kout, tokens), jnp.bfloat16),
        pltpu.VMEM((queries, tokens), jnp.bfloat16),
    ]
    if fold * per < kout:
        scratch.append(pltpu.VMEM((queries, rows), jnp.float32))
    return pl.pallas_call(
        functools.partial(
            precond_kernel, kin=kin, kout=kout, per=per, fold=fold, queries=queries
        ),
        in_specs=[VMEM, VMEM],
        out_specs=VMEM,
        out_shape=jax.ShapeDtypeStruct((queries, rows), jnp.bfloat16),
        scratch_shapes=scratch,
        compiler_params=pltpu.CompilerParams(vmem_limit_bytes=16 << 20),
        cost_estimate=pl.CostEstimate(
            flops=2 * queries * rows * coords,
            bytes_accessed=2 * rows * coords,
            transcendentals=0,
        ),
        name="precondition",
    )(tok, inverse)


def example_member(ids, examples):
    example = lax.broadcasted_iota(jnp.int32, (examples, ids.shape[1]), 0)
    return jnp.where(example == ids[...], 1.0, 0.0)


def near_kernel(near, stored, ids, part, sums, *, near_masks, far_masks, axis):
    me = lax.axis_index(axis)
    rows, examples = near.shape[2], part.shape[0]
    member = example_member(ids, examples)
    scores = jnp.zeros((stored.shape[0], near.shape[1]), jnp.float32)
    for n, mask in enumerate(near_masks):
        start = pl.multiple_of((me ^ mask) * rows, rows)
        scores += lax.dot_general(
            stored[:, pl.ds(start, rows)], near[n], NT, preferred_element_type=jnp.float32
        )
    part[...] = jnp.dot(
        member, scores, precision=lax.Precision.HIGHEST, preferred_element_type=jnp.float32
    )
    for n, mask in enumerate(far_masks):
        start = pl.multiple_of((me ^ mask) * rows, rows)
        total = jnp.dot(
            member.astype(jnp.bfloat16),
            stored[:, pl.ds(start, rows)],
            preferred_element_type=jnp.float32,
        )
        high = total.astype(jnp.bfloat16)
        sums[:examples, n * rows : (n + 1) * rows] = high
        sums[examples:, n * rows : (n + 1) * rows] = (
            total - high.astype(jnp.float32)
        ).astype(jnp.bfloat16)


def far_kernel(far, part, sums, out):
    rows, examples = far.shape[2], out.shape[0]
    total = jnp.zeros((2 * examples, out.shape[1]), jnp.float32)
    for n in range(far.shape[0]):
        total += lax.dot_general(
            sums[:, n * rows : (n + 1) * rows], far[n], NT, preferred_element_type=jnp.float32
        )
    out[...] = part[...] + total[:examples] + total[examples:]


def score_near(near, stored, ids, near_masks, far_masks):
    blocks, queries, rows = near.shape
    return pl.pallas_call(
        functools.partial(
            near_kernel, near_masks=near_masks, far_masks=far_masks, axis="rows"
        ),
        in_specs=[VMEM] * 3,
        out_specs=[VMEM] * 2,
        out_shape=[
            jax.ShapeDtypeStruct((EX_DEV, queries), jnp.float32),
            jax.ShapeDtypeStruct((2 * EX_DEV, blocks * rows), jnp.bfloat16),
        ],
        compiler_params=pltpu.CompilerParams(vmem_limit_bytes=8 << 20),
        cost_estimate=pl.CostEstimate(
            flops=stored.size * queries, bytes_accessed=stored.size, transcendentals=0
        ),
        name="score_near",
    )(near, stored, ids)


def score_far(far, part, sums):
    return pl.pallas_call(
        far_kernel,
        in_specs=[VMEM] * 3,
        out_specs=VMEM,
        out_shape=jax.ShapeDtypeStruct(part.shape, jnp.float32),
        compiler_params=pltpu.CompilerParams(vmem_limit_bytes=8 << 20),
        cost_estimate=pl.CostEstimate(
            flops=2 * sums.size * part.shape[1], bytes_accessed=2 * sums.size, transcendentals=0
        ),
        name="score_far",
    )(far, part, sums)


def rounds_of(n):
    bits = []
    bit = n // 2
    while bit > 1:
        bits.append(bit)
        bit //= 2
    rounds = [[bits[0] | 1]] if bits else []
    for k in range(1, len(bits), 2):
        pair = bits[k : k + 2]
        rounds.append([m | 1 for m in ([sum(pair)] if len(pair) == 2 else []) + pair])
    return rounds + [[1]]


def swap(x, mask, n):
    return lax.ppermute(x, "rows", [(i, i ^ mask) for i in range(n)])


def spread(x, held, masks, n):
    pieces = [x] + [swap(x, mask, n) for mask in masks]
    held = held + [h ^ mask for mask in masks for h in held]
    return jnp.concatenate(pieces, axis=0), held


def on_device(
    in_acts, out_grads, in_projection, out_projection, inverse, stored_rows, query_ids, example_ids
):
    n = lax.axis_size("rows")
    queries = QRY_DEV * n
    kin, kout = in_projection.shape[0], out_projection.shape[0]
    tok = project(
        in_acts, out_grads, in_projection, out_projection, query_ids[None, :], queries
    )
    *rounds, (last,) = rounds_of(n)
    for masks in rounds:
        tok, _ = spread(tok, [0], masks, n)
    tok, _ = spread(tok, [0], [last], n)
    near, held = precondition(tok, inverse, kin, kout, queries)[None], [0]
    for masks in rounds:
        near, held = spread(near, held, masks, n)
    far = swap(near, last, n)
    part, sums = score_near(near, stored_rows, example_ids, held, [h ^ last for h in held])
    return score_far(far, part, sums)


def solution(mesh):
    placed = (
        P(("groups", "rows"), None),
        P(("groups", "rows"), None),
        P(),
        P(),
        P("rows", None),
        P(("groups", "rows"), None),
        P(("groups", "rows")),
        P(("groups", "rows"), None),
    )
    return jax.shard_map(
        on_device,
        mesh=mesh,
        in_specs=placed,
        out_specs=P(("groups", "rows"), None),
        check_vma=False,
    )
```

```python
import functools

import jax
import jax.numpy as jnp
from jax import lax
from jax.experimental import pallas as pl
from jax.experimental.pallas import tpu as pltpu
from jax.sharding import PartitionSpec as P


LANES = 128
QRY_DEV = 1
EX_DEV = 16
NT = (((1,), (1,)), ((), ()))
VMEM = pl.BlockSpec(memory_space=pltpu.VMEM)
ANY = pl.BlockSpec(memory_space=pl.ANY)
PROJECT_VMEM = 56_543_328


def chunk_of(total, most):
    size = most
    while total % size:
        size //= 2
    return size


def round_up(n, m):
    return -(-n // m) * m


def portions(total, weights):
    unit = 2 * LANES
    cuts = [total * sum(weights[:k]) // sum(weights) // unit * unit for k in range(len(weights))]
    cuts.append(total)
    return [(lo, hi - lo) for lo, hi in zip(cuts, cuts[1:])]


def project_kernel(acts, grads, in_w, out_w, raw, acts_v, grads_v, in_v, out_v, sem, *, steps):
    copies = []
    for n, (own, other) in enumerate(steps):
        parts = ((grads, grads_v, other), (out_w, out_v, other), (acts, acts_v, own), (in_w, in_v, own))
        copies.append(
            [
                pltpu.make_async_copy(
                    src.at[:, pl.ds(start, size)], dst.at[:, pl.ds(start, size)], sem.at[n, k]
                )
                for k, (src, dst, (start, size)) in enumerate(parts)
            ]
        )
    for step in copies:
        for copy in step:
            copy.start()

    def product(x, w, start, size):
        return lax.dot_general(
            x[:, start : start + size],
            w[:, start : start + size],
            NT,
            preferred_element_type=jnp.float32,
        )

    kin = in_w.shape[0]
    in_sum, out_sum = [], []
    for n, ((start, size), other) in enumerate(steps):
        for copy in copies[n]:
            copy.wait()
        half = size // 2
        in_sum += [
            product(acts_v, in_v, start, half),
            product(acts_v, in_v, start + half, size - half),
        ]
        out_sum.append(product(grads_v, out_v, *other))
    raw[:, :kin] = sum(in_sum[1:], in_sum[0]).astype(jnp.bfloat16)
    raw[:, kin:] = sum(out_sum[1:], out_sum[0]).astype(jnp.bfloat16)


def mark_kernel(raw, ids, tok):
    tokens, done = raw.shape
    row = lax.broadcasted_iota(jnp.int32, (tokens, tokens), 0)
    col = lax.broadcasted_iota(jnp.int32, (tokens, tokens), 1)
    mine = jnp.sum(jnp.where(row == col, ids[...], 0), axis=1, keepdims=True)
    query = lax.broadcasted_iota(jnp.int32, (tokens, tok.shape[1] - done), 1)
    tok[:, :done] = raw[...]
    tok[:, done:] = jnp.where(query == mine, 1.0, 0.0).astype(jnp.bfloat16)


def project(acts, grads, in_w, out_w, ids, queries):
    tokens, ff = acts.shape
    steps = list(zip(portions(ff, (2, 2, 2, 1)), portions(grads.shape[1], (1, 1, 1, 1))))
    width = in_w.shape[0] + out_w.shape[0]
    raw = pl.pallas_call(
        functools.partial(project_kernel, steps=steps),
        in_specs=[ANY] * 4,
        out_specs=VMEM,
        out_shape=jax.ShapeDtypeStruct((tokens, width), jnp.bfloat16),
        scratch_shapes=[
            pltpu.VMEM(acts.shape, acts.dtype),
            pltpu.VMEM(grads.shape, grads.dtype),
            pltpu.VMEM(in_w.shape, in_w.dtype),
            pltpu.VMEM(out_w.shape, out_w.dtype),
            pltpu.SemaphoreType.DMA((len(steps), 4)),
        ],
        compiler_params=pltpu.CompilerParams(vmem_limit_bytes=PROJECT_VMEM),
        name="project",
    )(acts, grads, in_w, out_w)
    return pl.pallas_call(
        mark_kernel,
        in_specs=[VMEM, VMEM],
        out_specs=VMEM,
        out_shape=jax.ShapeDtypeStruct(
            (tokens, width + round_up(queries, LANES)), jnp.bfloat16
        ),
        compiler_params=pltpu.CompilerParams(vmem_limit_bytes=2 << 20),
        cost_estimate=pl.CostEstimate(
            flops=10**11, bytes_accessed=10**8, transcendentals=0
        ),
        name="mark",
    )(raw, ids)


def precond_kernel(tok, inverse, out, out_t, member_t, *acc, kin, kout, per, fold, queries):
    out_t[...] = tok[:, kin : kin + kout].astype(jnp.float32).T.astype(jnp.bfloat16)
    member_t[...] = (
        tok[:, kin + kout :].astype(jnp.float32).T[:queries].astype(jnp.bfloat16)
    )

    def grads(first):
        o = out_t[pl.ds(first, per), :]
        weighted = (o[:, None, :] * member_t[...][None, :, :]).reshape(per * queries, o.shape[1])
        g = jnp.dot(weighted, tok[:, :kin], preferred_element_type=jnp.float32)
        g = g.astype(jnp.bfloat16)
        return [g[k * queries : (k + 1) * queries] for k in range(per)]

    def product(first):
        g = []
        for n in range(fold):
            g += grads(first + n * per)
        start = first * kin if isinstance(first, int) else pl.multiple_of(first * kin, kin)
        block = inverse[:, pl.ds(start, fold * per * kin)]
        return lax.dot_general(
            jnp.concatenate(g, axis=1), block, NT, preferred_element_type=jnp.float32
        )

    if not acc:
        out[...] = product(0).astype(jnp.bfloat16)
        return
    total = acc[0]
    total[...] = jnp.zeros_like(total)

    def step(s):
        total[...] += product(s * (fold * per))

    pl.loop(0, kout // (fold * per))(step)
    out[...] = total[...].astype(jnp.bfloat16)


def precondition(tok, inverse, kin, kout, queries):
    rows, coords = inverse.shape
    tokens = tok.shape[0]
    per = chunk_of(kout, max(8, (1 << 16) // (queries * tokens)))
    fold = chunk_of(kout // per, max(1, (1 << 18) // (per * queries * tokens) * 2))
    scratch = [
        pltpu.VMEM((kout, tokens), jnp.bfloat16),
        pltpu.VMEM((queries, tokens), jnp.bfloat16),
    ]
    if fold * per < kout:
        scratch.append(pltpu.VMEM((queries, rows), jnp.float32))
    return pl.pallas_call(
        functools.partial(
            precond_kernel, kin=kin, kout=kout, per=per, fold=fold, queries=queries
        ),
        in_specs=[VMEM, VMEM],
        out_specs=VMEM,
        out_shape=jax.ShapeDtypeStruct((queries, rows), jnp.bfloat16),
        scratch_shapes=scratch,
        compiler_params=pltpu.CompilerParams(vmem_limit_bytes=16 << 20),
        cost_estimate=pl.CostEstimate(
            flops=2 * queries * rows * coords,
            bytes_accessed=2 * rows * coords,
            transcendentals=0,
        ),
        name="precondition",
    )(tok, inverse)


def example_member(ids, examples):
    example = lax.broadcasted_iota(jnp.int32, (examples, ids.shape[1]), 0)
    return jnp.where(example == ids[...], 1.0, 0.0)


def near_kernel(*refs, near_masks, far_masks, axis):
    *held, stored, ids, part, sums = refs
    me = lax.axis_index(axis)
    rows, examples = held[0].shape[2], part.shape[0]
    member = example_member(ids, examples)
    scores = jnp.zeros((stored.shape[0], part.shape[1]), jnp.float32)
    blocks = [ref.at[n] for ref in held for n in range(ref.shape[0])]
    for block, mask in zip(blocks, near_masks, strict=True):
        start = pl.multiple_of((me ^ mask) * rows, rows)
        scores += lax.dot_general(
            stored[:, pl.ds(start, rows)], block[...], NT, preferred_element_type=jnp.float32
        )
    part[...] = jnp.dot(
        member, scores, precision=lax.Precision.HIGHEST, preferred_element_type=jnp.float32
    )
    for n, mask in enumerate(far_masks):
        start = pl.multiple_of((me ^ mask) * rows, rows)
        total = jnp.dot(
            member.astype(jnp.bfloat16),
            stored[:, pl.ds(start, rows)],
            preferred_element_type=jnp.float32,
        )
        high = total.astype(jnp.bfloat16)
        sums[:examples, n * rows : (n + 1) * rows] = high
        sums[examples:, n * rows : (n + 1) * rows] = (
            total - high.astype(jnp.float32)
        ).astype(jnp.bfloat16)


def far_kernel(far, part, sums, out):
    rows, examples = far.shape[2], out.shape[0]
    total = jnp.zeros((2 * examples, out.shape[1]), jnp.float32)
    for n in range(far.shape[0]):
        total += lax.dot_general(
            sums[:, n * rows : (n + 1) * rows], far[n], NT, preferred_element_type=jnp.float32
        )
    out[...] = part[...] + total[:examples] + total[examples:]


def score_near(held, stored, ids, near_masks, far_masks):
    _, queries, rows = held[0].shape
    return pl.pallas_call(
        functools.partial(
            near_kernel, near_masks=near_masks, far_masks=far_masks, axis="rows"
        ),
        in_specs=[VMEM] * (len(held) + 2),
        out_specs=[VMEM] * 2,
        out_shape=[
            jax.ShapeDtypeStruct((EX_DEV, queries), jnp.float32),
            jax.ShapeDtypeStruct((2 * EX_DEV, len(far_masks) * rows), jnp.bfloat16),
        ],
        compiler_params=pltpu.CompilerParams(vmem_limit_bytes=8 << 20),
        cost_estimate=pl.CostEstimate(
            flops=stored.size * queries, bytes_accessed=stored.size, transcendentals=0
        ),
        name="score_near",
    )(*held, stored, ids)


def score_far(far, part, sums):
    return pl.pallas_call(
        far_kernel,
        in_specs=[VMEM] * 3,
        out_specs=VMEM,
        out_shape=jax.ShapeDtypeStruct(part.shape, jnp.float32),
        compiler_params=pltpu.CompilerParams(vmem_limit_bytes=8 << 20),
        cost_estimate=pl.CostEstimate(
            flops=2 * sums.size * part.shape[1], bytes_accessed=2 * sums.size, transcendentals=0
        ),
        name="score_far",
    )(far, part, sums)


def rounds_of(n):
    bits = []
    bit = n // 2
    while bit > 1:
        bits.append(bit)
        bit //= 2
    rounds = [[bits[0] | 1]] if bits else []
    for k in range(1, len(bits), 2):
        pair = bits[k : k + 2]
        rounds.append([m | 1 for m in ([sum(pair)] if len(pair) == 2 else []) + pair])
    return rounds + [[1]]


def swap(x, mask, n):
    return lax.ppermute(x, "rows", [(i, i ^ mask) for i in range(n)])


def spread(x, held, masks, n):
    pieces = [x] + [swap(x, mask, n) for mask in masks]
    held = held + [h ^ mask for mask in masks for h in held]
    return jnp.concatenate(pieces, axis=0), held


def on_device(
    in_acts, out_grads, in_projection, out_projection, inverse, stored_rows, query_ids, example_ids
):
    n = lax.axis_size("rows")
    queries = QRY_DEV * n
    kin, kout = in_projection.shape[0], out_projection.shape[0]
    tok = project(
        in_acts, out_grads, in_projection, out_projection, query_ids[None, :], queries
    )
    *rounds, (last,) = rounds_of(n)
    for masks in rounds:
        tok, _ = spread(tok, [0], masks, n)
    tok = jnp.concatenate([tok, swap(tok, last, n)], axis=0)
    near, held = precondition(tok, inverse, kin, kout, queries)[None], [0]
    for masks in rounds[:-1]:
        near, held = spread(near, held, masks, n)
    masks = rounds[-1]
    pieces = [swap(near, mask, n) for mask in masks]
    first = len(masks) // 2
    early = jnp.concatenate([near] + pieces[:first], axis=0)
    late = jnp.concatenate(pieces[first:], axis=0)
    early_held = held + [h ^ mask for mask in masks[:first] for h in held]
    late_held = [h ^ mask for mask in masks[first:] for h in held]
    across = swap(early, last, n)
    far = swap(late, last, n)
    part, sums = score_near(
        [early, late, across],
        stored_rows,
        example_ids,
        early_held + late_held + [h ^ last for h in early_held],
        [h ^ last for h in late_held],
    )
    return score_far(far, part, sums)


def solution(mesh):
    placed = (
        P(("groups", "rows"), None),
        P(("groups", "rows"), None),
        P(),
        P(),
        P("rows", None),
        P(("groups", "rows"), None),
        P(("groups", "rows")),
        P(("groups", "rows"), None),
    )

    return jax.shard_map(
        on_device,
        mesh=mesh,
        in_specs=placed,
        out_specs=P(("groups", "rows"), None),
        check_vma=False,
    )
```

```python
import functools

import jax
import jax.numpy as jnp
from jax import lax
from jax.experimental import pallas as pl
from jax.experimental.pallas import tpu as pltpu
from jax.sharding import PartitionSpec as P


LANES = 128
QRY_DEV = 1
EX_DEV = 16
NT = (((1,), (1,)), ((), ()))
VMEM = pl.BlockSpec(memory_space=pltpu.VMEM)
ANY = pl.BlockSpec(memory_space=pl.ANY)
PROJECT_VMEM = 56_543_328


def chunk_of(total, most):
    size = most
    while total % size:
        size //= 2
    return size


def round_up(n, m):
    return -(-n // m) * m


def portions(total, weights):
    unit = 2 * LANES
    cuts = [total * sum(weights[:k]) // sum(weights) // unit * unit for k in range(len(weights))]
    cuts.append(total)
    return [(lo, hi - lo) for lo, hi in zip(cuts, cuts[1:])]


def project_kernel(acts, grads, in_w, out_w, raw, acts_v, grads_v, in_v, out_v, sem, *, steps):
    copies = []
    for n, (own, other) in enumerate(steps):
        parts = ((grads, grads_v, other), (out_w, out_v, other), (acts, acts_v, own), (in_w, in_v, own))
        copies.append(
            [
                pltpu.make_async_copy(
                    src.at[:, pl.ds(start, size)], dst.at[:, pl.ds(start, size)], sem.at[n, k]
                )
                for k, (src, dst, (start, size)) in enumerate(parts)
            ]
        )
    for step in copies:
        for copy in step:
            copy.start()

    def product(x, w, start, size):
        return lax.dot_general(
            x[:, start : start + size],
            w[:, start : start + size],
            NT,
            preferred_element_type=jnp.float32,
        )

    kin = in_w.shape[0]
    in_sum, out_sum = [], []
    for n, ((start, size), other) in enumerate(steps):
        for copy in copies[n]:
            copy.wait()
        half = size // 2
        in_sum += [
            product(acts_v, in_v, start, half),
            product(acts_v, in_v, start + half, size - half),
        ]
        out_sum.append(product(grads_v, out_v, *other))
    raw[:, :kin] = sum(in_sum[1:], in_sum[0]).astype(jnp.bfloat16)
    raw[:, kin:] = sum(out_sum[1:], out_sum[0]).astype(jnp.bfloat16)


def mark_kernel(raw, ids, tok):
    tokens, done = raw.shape
    row = lax.broadcasted_iota(jnp.int32, (tokens, tokens), 0)
    col = lax.broadcasted_iota(jnp.int32, (tokens, tokens), 1)
    mine = jnp.sum(jnp.where(row == col, ids[...], 0), axis=1, keepdims=True)
    query = lax.broadcasted_iota(jnp.int32, (tokens, tok.shape[1] - done), 1)
    tok[:, :done] = raw[...]
    tok[:, done:] = jnp.where(query == mine, 1.0, 0.0).astype(jnp.bfloat16)


def project(acts, grads, in_w, out_w, ids, queries):
    tokens, ff = acts.shape
    steps = list(zip(portions(ff, (2, 2, 2, 1)), portions(grads.shape[1], (1, 1, 1, 1))))
    width = in_w.shape[0] + out_w.shape[0]
    raw = pl.pallas_call(
        functools.partial(project_kernel, steps=steps),
        in_specs=[ANY] * 4,
        out_specs=VMEM,
        out_shape=jax.ShapeDtypeStruct((tokens, width), jnp.bfloat16),
        scratch_shapes=[
            pltpu.VMEM(acts.shape, acts.dtype),
            pltpu.VMEM(grads.shape, grads.dtype),
            pltpu.VMEM(in_w.shape, in_w.dtype),
            pltpu.VMEM(out_w.shape, out_w.dtype),
            pltpu.SemaphoreType.DMA((len(steps), 4)),
        ],
        compiler_params=pltpu.CompilerParams(vmem_limit_bytes=PROJECT_VMEM),
        name="project",
    )(acts, grads, in_w, out_w)
    return pl.pallas_call(
        mark_kernel,
        in_specs=[VMEM, VMEM],
        out_specs=VMEM,
        out_shape=jax.ShapeDtypeStruct(
            (tokens, width + round_up(queries, LANES)), jnp.bfloat16
        ),
        compiler_params=pltpu.CompilerParams(vmem_limit_bytes=2 << 20),
        cost_estimate=pl.CostEstimate(
            flops=10**11, bytes_accessed=10**8, transcendentals=0
        ),
        name="mark",
    )(raw, ids)


def precond_kernel(tok, inverse, out, out_t, member_t, *acc, kin, kout, per, fold, queries):
    out_t[...] = tok[:, kin : kin + kout].astype(jnp.float32).T.astype(jnp.bfloat16)
    member_t[...] = (
        tok[:, kin + kout :].astype(jnp.float32).T[:queries].astype(jnp.bfloat16)
    )

    def grads(first):
        o = out_t[pl.ds(first, per), :]
        weighted = (o[:, None, :] * member_t[...][None, :, :]).reshape(per * queries, o.shape[1])
        g = jnp.dot(weighted, tok[:, :kin], preferred_element_type=jnp.float32)
        g = g.astype(jnp.bfloat16)
        return [g[k * queries : (k + 1) * queries] for k in range(per)]

    def product(first):
        g = []
        for n in range(fold):
            g += grads(first + n * per)
        start = first * kin if isinstance(first, int) else pl.multiple_of(first * kin, kin)
        block = inverse[:, pl.ds(start, fold * per * kin)]
        return lax.dot_general(
            jnp.concatenate(g, axis=1), block, NT, preferred_element_type=jnp.float32
        )

    if not acc:
        out[...] = product(0).astype(jnp.bfloat16)
        return
    total = acc[0]
    total[...] = jnp.zeros_like(total)

    def step(s):
        total[...] += product(s * (fold * per))

    pl.loop(0, kout // (fold * per))(step)
    out[...] = total[...].astype(jnp.bfloat16)


def precondition(tok, inverse, kin, kout, queries):
    rows, coords = inverse.shape
    tokens = tok.shape[0]
    per = chunk_of(kout, max(8, (1 << 16) // (queries * tokens)))
    fold = chunk_of(kout // per, max(1, (1 << 18) // (per * queries * tokens) * 2))
    scratch = [
        pltpu.VMEM((kout, tokens), jnp.bfloat16),
        pltpu.VMEM((queries, tokens), jnp.bfloat16),
    ]
    if fold * per < kout:
        scratch.append(pltpu.VMEM((queries, rows), jnp.float32))
    return pl.pallas_call(
        functools.partial(
            precond_kernel, kin=kin, kout=kout, per=per, fold=fold, queries=queries
        ),
        in_specs=[VMEM, VMEM],
        out_specs=VMEM,
        out_shape=jax.ShapeDtypeStruct((queries, rows), jnp.bfloat16),
        scratch_shapes=scratch,
        compiler_params=pltpu.CompilerParams(vmem_limit_bytes=16 << 20),
        cost_estimate=pl.CostEstimate(
            flops=2 * queries * rows * coords,
            bytes_accessed=2 * rows * coords,
            transcendentals=0,
        ),
        name="precondition",
    )(tok, inverse)


def example_member(ids, examples):
    example = lax.broadcasted_iota(jnp.int32, (examples, ids.shape[1]), 0)
    return jnp.where(example == ids[...], 1.0, 0.0)


def near_kernel(*refs, near_masks, far_masks, axis):
    *held, stored, ids, part, sums = refs
    me = lax.axis_index(axis)
    rows, examples = held[0].shape[2], part.shape[0]
    member = example_member(ids, examples)
    scores = jnp.zeros((stored.shape[0], part.shape[1]), jnp.float32)
    blocks = [ref.at[n] for ref in held for n in range(ref.shape[0])]
    for block, mask in zip(blocks, near_masks, strict=True):
        start = pl.multiple_of((me ^ mask) * rows, rows)
        scores += lax.dot_general(
            stored[:, pl.ds(start, rows)], block[...], NT, preferred_element_type=jnp.float32
        )
    part[...] = jnp.dot(
        member, scores, precision=lax.Precision.HIGHEST, preferred_element_type=jnp.float32
    )
    for n, mask in enumerate(far_masks):
        start = pl.multiple_of((me ^ mask) * rows, rows)
        total = jnp.dot(
            member.astype(jnp.bfloat16),
            stored[:, pl.ds(start, rows)],
            preferred_element_type=jnp.float32,
        )
        high = total.astype(jnp.bfloat16)
        sums[:examples, n * rows : (n + 1) * rows] = high
        sums[examples:, n * rows : (n + 1) * rows] = (
            total - high.astype(jnp.float32)
        ).astype(jnp.bfloat16)


def far_kernel(far, part, sums, out):
    rows, examples = far.shape[2], out.shape[0]
    total = jnp.zeros((2 * examples, out.shape[1]), jnp.float32)
    for n in range(far.shape[0]):
        total += lax.dot_general(
            sums[:, n * rows : (n + 1) * rows], far[n], NT, preferred_element_type=jnp.float32
        )
    out[...] = part[...] + total[:examples] + total[examples:]


def score_near(held, stored, ids, near_masks, far_masks):
    _, queries, rows = held[0].shape
    return pl.pallas_call(
        functools.partial(
            near_kernel, near_masks=near_masks, far_masks=far_masks, axis="rows"
        ),
        in_specs=[VMEM] * (len(held) + 2),
        out_specs=[VMEM] * 2,
        out_shape=[
            jax.ShapeDtypeStruct((EX_DEV, queries), jnp.float32),
            jax.ShapeDtypeStruct((2 * EX_DEV, len(far_masks) * rows), jnp.bfloat16),
        ],
        compiler_params=pltpu.CompilerParams(vmem_limit_bytes=8 << 20),
        cost_estimate=pl.CostEstimate(
            flops=stored.size * queries, bytes_accessed=stored.size, transcendentals=0
        ),
        name="score_near",
    )(*held, stored, ids)


def score_far(far, part, sums):
    return pl.pallas_call(
        far_kernel,
        in_specs=[VMEM] * 3,
        out_specs=VMEM,
        out_shape=jax.ShapeDtypeStruct(part.shape, jnp.float32),
        compiler_params=pltpu.CompilerParams(vmem_limit_bytes=8 << 20),
        cost_estimate=pl.CostEstimate(
            flops=2 * sums.size * part.shape[1], bytes_accessed=2 * sums.size, transcendentals=0
        ),
        name="score_far",
    )(far, part, sums)


def rounds_of(n):
    bits = []
    bit = n // 2
    while bit > 1:
        bits.append(bit)
        bit //= 2
    rounds = [[bits[0] | 1]] if bits else []
    for k in range(1, len(bits), 2):
        pair = bits[k : k + 2]
        rounds.append([m | 1 for m in ([sum(pair)] if len(pair) == 2 else []) + pair])
    return rounds + [[1]]


def swap(x, mask, n):
    return lax.ppermute(x, "rows", [(i, i ^ mask) for i in range(n)])


def spread(x, held, masks, n):
    pieces = [x] + [swap(x, mask, n) for mask in masks]
    held = held + [h ^ mask for mask in masks for h in held]
    return jnp.concatenate(pieces, axis=0), held


def on_device(
    in_acts, out_grads, in_projection, out_projection, inverse, stored_rows, query_ids, example_ids
):
    n = lax.axis_size("rows")
    queries = QRY_DEV * n
    kin, kout = in_projection.shape[0], out_projection.shape[0]
    tok = project(
        in_acts, out_grads, in_projection, out_projection, query_ids[None, :], queries
    )
    *rounds, (last,) = rounds_of(n)
    for masks in rounds[:-1]:
        tok, _ = spread(tok, [0], masks, n)
    masks = rounds[-1]
    pieces = [swap(tok, mask, n) for mask in masks]
    first = len(masks) // 2
    early = jnp.concatenate([tok] + pieces[:first], axis=0)
    late = jnp.concatenate(pieces[first:], axis=0)
    across = swap(early, last, n)
    tok = jnp.concatenate([early, late, across, swap(late, last, n)], axis=0)
    near, held = precondition(tok, inverse, kin, kout, queries)[None], [0]
    for masks in rounds[:-1]:
        near, held = spread(near, held, masks, n)
    masks = rounds[-1]
    pieces = [swap(near, mask, n) for mask in masks]
    first = len(masks) // 2
    early = jnp.concatenate([near] + pieces[:first], axis=0)
    late = jnp.concatenate(pieces[first:], axis=0)
    early_held = held + [h ^ mask for mask in masks[:first] for h in held]
    late_held = [h ^ mask for mask in masks[first:] for h in held]
    across = swap(early, last, n)
    far = swap(late, last, n)
    part, sums = score_near(
        [early, late, across],
        stored_rows,
        example_ids,
        early_held + late_held + [h ^ last for h in early_held],
        [h ^ last for h in late_held],
    )
    return score_far(far, part, sums)


def solution(mesh):
    placed = (
        P(("groups", "rows"), None),
        P(("groups", "rows"), None),
        P(),
        P(),
        P("rows", None),
        P(("groups", "rows"), None),
        P(("groups", "rows")),
        P(("groups", "rows"), None),
    )

    return jax.shard_map(
        on_device,
        mesh=mesh,
        in_specs=placed,
        out_specs=P(("groups", "rows"), None),
        check_vma=False,
    )
```
